32 devices in a mesh: row: 4 (over z), col: 8 (over y, x, core).
Axes of the slice: x: 2, y: 2, z: 4, core: 2. Of those that a mesh axis runs over, the one named last changes fastest.
Arguments:
- inverse_block: float32 [512, 512], P('row', 'col'), as said below
- panels: bfloat16 [2, 512, 512], P(None, 'row'), may hold values from -0.375 to 0.375
- pattern: int32 [2, 4], replicated, may hold values 0 or 1
Outputs:
- inverse_panel: float32 [2, 512, 512], P(None, ('row', 'col'))
- update: float32 [2, 512, 512], P(None, 'col')
The draws below stay inside these ranges and needn't reach their ends.
Inputs may be any that keep to these rules, and one draw needn't show every extreme that they name: `pattern`: 1 marks a block of rows in the supernode's structure, 0 a block outside it. `inverse_block`: symmetric.
All inputs are finite; a program needn't handle non-finite values.
Results may differ from the reference program's by a relative error of at most 0.00045.
Values may be sent and summed in bfloat16 or wider, within the bound.
No kernel may reach another device: no remote copies, remote signals or barrier semaphores. Data moves between devices by JAX's collectives and lax.ppermute only.
A program may use at most 64 MiB of HBM per device.

```python
import jax
import jax.numpy as jnp
from jax import lax

W = 512
BLOCK = 128
NA = 512
NB = 4


def draw_inverse_block(key, part):
    key_rough = jax.random.fold_in(key, 11)
    key_diag = jax.random.fold_in(key, 12)
    rough = jax.random.normal(key_rough, (NA, NA), jnp.float32)
    sym = (rough + rough.T) * (0.35 / NA ** 0.5)
    diag_vals = jax.random.uniform(key_diag, (NA,), jnp.float32, 1.0, 2.0)
    return sym + jnp.diag(diag_vals)


def touch_ends(drawn, stream_key, smallest, high):
    spot = [jax.random.randint(jax.random.fold_in(stream_key, axis), (), 0, length) for axis, length in enumerate(drawn.shape)]
    longest = drawn.shape.index(max(drawn.shape))
    next_to = spot[:longest] + [(spot[longest] + 1) % drawn.shape[longest]] + spot[longest + 1:]
    return drawn.at[tuple(spot)].set(smallest).at[tuple(next_to)].set(high)


def level_of(rng, extent, split, least, high):
    gain = 1.0
    for axis_at, blocks in split:
        draws = jax.random.uniform(jax.random.fold_in(jax.random.fold_in(rng, 6), axis_at), (blocks,), jnp.float32, least / len(split), high / len(split))
        gain = gain * jnp.repeat(jnp.exp(draws), extent[axis_at] // blocks).reshape((-1,) + (1,) * (len(extent) - 1 - axis_at))
    return gain


def scatter_about(stream_key, dims, scale, limit, cuts=(), kind=jnp.bfloat16):
    entries = scale * jax.random.normal(stream_key, dims, jnp.float32)
    if cuts:
        entries = entries * level_of(stream_key, dims, cuts, -0.22, 0.18)
    return jnp.clip(entries, -limit, limit).astype(kind)


def setup_inputs(seed: int = 0) -> dict:
    arg_keys = jax.random.split(jax.random.key(seed), 4)
    return {
        "inverse_block": draw_inverse_block(jax.random.fold_in(arg_keys[3], 71), 0),
        "panels": scatter_about(arg_keys[1], (2, NA, W), (NA // 2) ** -0.5, 0.375, ((1, 4),)),
        "pattern": touch_ends((jax.random.randint(arg_keys[2], (2, NB), 0, 2) < 1).astype(jnp.int32), jax.random.fold_in(arg_keys[2], 1), 0, 1),
    }


def reference(inverse_block, panels, pattern):
    block_ids = jnp.arange(NA, dtype=jnp.int32) // BLOCK
    onehot = block_ids[:, None] == jnp.arange(NB, dtype=jnp.int32)[None, :]
    row_mask = jnp.sum(jnp.where(onehot[None, :, :], pattern[:, None, :], 0), axis=2)
    used = panels * row_mask[:, :, None].astype(jnp.bfloat16)
    used_wide = used.astype(jnp.float32)
    product = jnp.einsum("ij,sjw->siw", inverse_block, used_wide, precision=lax.Precision.HIGHEST)
    inverse_panel = -(product * row_mask[:, :, None].astype(jnp.float32))
    update = -jnp.einsum("siv,siw->svw", used_wide, inverse_panel, precision=lax.Precision.HIGHEST)
    return inverse_panel, update
```

```python
import functools

import jax
import jax.numpy as jnp
from jax import lax
from jax.experimental import pallas as pl
from jax.experimental.pallas import tpu as pltpu
from jax.sharding import PartitionSpec as P


LANES = 128
LOCAL_BYTES = 4 << 20
KERNEL_VMEM = 16 << 20


def spread(block, axis, source):
    block = jnp.where(lax.axis_index(axis) == source, block, jnp.zeros_like(block))
    return lax.psum(block, axis)


def reducing(inverse_block, panels, pattern):
    row_count = lax.axis_size("row")
    col_count = lax.axis_size("col")
    row_index = lax.axis_index("row")
    col_index = lax.axis_index("col")
    rows_here = panels.shape[1]
    cols_here = inverse_block.shape[1]
    width = panels.shape[2]
    blocks = pattern.shape[1]
    block = rows_here * row_count // blocks
    ratio = col_count // row_count
    span = rows_here // col_count
    row_ids = row_index * rows_here + jnp.arange(rows_here, dtype=jnp.int32)
    onehot = (row_ids // block)[:, None] == jnp.arange(blocks, dtype=jnp.int32)[None, :]
    row_mask = jnp.sum(jnp.where(onehot[None, :, :], pattern[:, None, :], 0), axis=2)
    used = panels * row_mask[:, :, None].astype(jnp.bfloat16)
    piece = lax.dynamic_slice_in_dim(used, col_index % ratio * cols_here, cols_here, 1)
    col_panel = spread(piece, "row", col_index // ratio)
    product = jnp.einsum(
        "ij,sjw->siw", inverse_block, col_panel.astype(jnp.float32), precision=lax.Precision.HIGHEST
    )
    term = -(product * row_mask[:, :, None].astype(jnp.float32))
    share = width // col_count
    partial_update = jnp.einsum(
        "siv,siw->svw", used.astype(jnp.float32), term, precision=lax.Precision.HIGHEST
    )
    panel_parts = term.reshape(2, col_count, span, width)
    update_parts = partial_update.reshape(2, col_count, share, width)
    joined = jnp.concatenate([panel_parts, update_parts], axis=2).reshape(
        2, col_count * (span + share), width
    )
    received = lax.psum_scatter(joined, "col", scatter_dimension=1, tiled=True)
    inverse_panel = received[:, :span]
    update = -lax.psum(received[:, span:], "row")
    return (inverse_panel, update)


def halves(value):
    high = value.astype(jnp.bfloat16)
    return high, (value - high.astype(jnp.float32)).astype(jnp.bfloat16)


def pack_kernel(a_ref, panels_ref, a_out, panel_out):
    core = lax.axis_index("col") % 2
    a = a_ref[...]
    high = a.astype(jnp.bfloat16).astype(jnp.float32)
    a_out[...] = jnp.concatenate([high, a - high], axis=1).astype(jnp.bfloat16)
    panel_out[...] = panels_ref[core]


def local_kernel(
    row_count, col_count, pattern_ref, panels_ref, *refs
):
    near = refs[: row_count - 1]
    far = refs[row_count - 1 : 2 * (row_count - 1)]
    a_refs = refs[2 * (row_count - 1) : 2 * (row_count - 1) + col_count]
    inverse_out, update_out, used, y_t, lhs, picked = refs[2 * (row_count - 1) + col_count :]
    row = lax.axis_index("row")
    col = lax.axis_index("col")
    core = col % 2
    rows = panels_ref.shape[1]
    cols = a_refs[0].shape[1] // 2
    share = update_out.shape[1]
    span = inverse_out.shape[1]
    block = rows * row_count // pattern_ref.shape[1]

    def keep(s, d, ref, at):
        for start in range(0, rows, block):
            flag = pattern_ref[s, ((row ^ d) * rows + start) // block]
            value = ref[at + (pl.ds(start, block), slice(None))]
            used[s, pl.ds(d * rows + start, block), :] = jnp.where(
                flag != 0, value, jnp.zeros_like(value)
            )

    for s in range(2):
        keep(s, 0, panels_ref, (s,))
    for d in range(1, row_count):
        keep(core, d, near[d - 1], ())
        keep(1 - core, d, far[d - 1], ())

    lanes = pl.ds(pl.multiple_of(col // 2 * LANES, LANES), LANES)
    total = None
    for e in range(col_count):
        first = (col ^ e) * cols
        start = pl.multiple_of((row ^ (first // rows)) * rows + first % rows, cols)
        at = pl.ds(start, cols)
        rhs = jnp.concatenate([used[0, at, lanes], used[1, at, lanes]], axis=1)
        rhs = jnp.concatenate([rhs, rhs], axis=0)
        part = jnp.dot(a_refs[e][...], rhs, preferred_element_type=jnp.float32)
        total = part if total is None else total + part
    y_t[...] = total.T

    first = row * rows + col * span
    chosen = col ^ (first // cols)
    for e in range(col_count):

        @pl.when(chosen == e)
        def _():
            picked[...] = a_refs[e][...].astype(jnp.float32).T

    offset = pl.multiple_of(first % cols, span)
    lhs[pl.ds(2 * share, span), :] = picked[pl.ds(offset, span), :].astype(jnp.bfloat16)
    lhs[pl.ds(2 * share + span, span), :] = picked[pl.ds(cols + offset, span), :].astype(jnp.bfloat16)
    for s in range(2):
        mine = y_t[pl.ds(pl.multiple_of(s * LANES + core * share, share), share), :]
        high, low = halves(mine)
        lhs[pl.ds(0, share), :] = high
        lhs[pl.ds(share, share), :] = low
        out = jnp.dot(lhs[...], used[s], preferred_element_type=jnp.float32)
        update_out[s] = out[:share] + out[share : 2 * share]
        flag = pattern_ref[s, first // block]
        product = out[2 * share : 2 * share + span] + out[2 * share + span :]
        inverse_out[s] = jnp.where(flag != 0, -product, jnp.zeros_like(product))


def gathering(inverse_block, panels, pattern):
    row_count = lax.axis_size("row")
    col_count = lax.axis_size("col")
    _, rows, width = panels.shape
    cols = inverse_block.shape[1]
    height = rows * row_count
    share = width // col_count
    span = rows // col_count
    vmem = pl.BlockSpec(memory_space=pltpu.VMEM)
    params = pltpu.CompilerParams(vmem_limit_bytes=KERNEL_VMEM)

    def swap(value, axis, by):
        return lax.ppermute(value, axis, [(i, i ^ by) for i in range(lax.axis_size(axis))])

    a, panel = pl.pallas_call(
        pack_kernel,
        out_shape=(
            jax.ShapeDtypeStruct((rows, 2 * cols), jnp.bfloat16),
            jax.ShapeDtypeStruct((rows, width), jnp.bfloat16),
        ),
        in_specs=[vmem] * 2,
        out_specs=(vmem,) * 2,
        compiler_params=params,
    )(inverse_block, panels)
    a_rows = [a] + [swap(a, "row", d) for d in range(1, row_count)]
    near = [swap(panel, "row", d) for d in range(1, row_count)]
    far = [swap(p, "col", 1) for p in near]
    a_col = jnp.concatenate(a_rows, axis=0)
    even = [a_col] + [swap(a_col, "col", e) for e in range(2, col_count, 2)]
    a_all = []
    for value in even:
        a_all += [value, swap(value, "col", 1)]
    return pl.pallas_call(
        functools.partial(local_kernel, row_count, col_count),
        out_shape=(
            jax.ShapeDtypeStruct((2, span, width), jnp.float32),
            jax.ShapeDtypeStruct((2, share, width), jnp.float32),
        ),
        in_specs=[pl.BlockSpec(memory_space=pltpu.SMEM)] + [vmem] * (1 + 2 * (row_count - 1) + col_count),
        out_specs=(vmem,) * 2,
        scratch_shapes=[
            pltpu.VMEM((2, height, width), jnp.bfloat16),
            pltpu.VMEM((2 * LANES, height), jnp.float32),
            pltpu.VMEM((2 * share + 2 * span, height), jnp.bfloat16),
            pltpu.VMEM((2 * cols, height), jnp.float32),
        ],
        compiler_params=params,
    )(pattern, panels, *near, *far, *a_all)


def fits(mesh, inverse_block, panels, pattern):
    row_count, col_count = mesh.shape["row"], mesh.shape["col"]
    height, width = inverse_block.shape[0], panels.shape[2]
    rows, cols = height // row_count, height // col_count
    block = height // pattern.shape[1]
    powers = all(n & (n - 1) == 0 for n in (row_count, col_count))
    return (
        powers
        and col_count > 1
        and inverse_block.size * 4 <= LOCAL_BYTES
        and 2 * cols == LANES
        and 2 * (width // col_count) == LANES
        and rows % cols == 0
        and rows % block == 0
        and block % 16 == 0
        and (rows // col_count) % 16 == 0
    )


def solution(mesh):
    def run(inverse_block, panels, pattern):
        body = gathering if fits(mesh, inverse_block, panels, pattern) else reducing
        return jax.shard_map(
            body,
            mesh=mesh,
            in_specs=(P("row", "col"), P(None, "row", None), P()),
            out_specs=(P(None, ("row", "col"), None), P(None, "col", None)),
            check_vma=False,
        )(inverse_block, panels, pattern)

    return run
```

```python
import jax
import jax.numpy as jnp
from jax import lax
from jax.experimental import pallas as pl
from jax.experimental.pallas import tpu as pltpu
from jax.sharding import PartitionSpec as P


LANES = 128
LOCAL_BYTES = 4 << 20
KERNEL_VMEM = 16 << 20
PACK_PARAMS = pltpu.CompilerParams(vmem_limit_bytes=KERNEL_VMEM)
SECOND = {1: 3, 2: 1, 3: 2}
SOURCE = {by ^ second: by for by, second in SECOND.items()}


def spread(block, axis, source):
    block = jnp.where(lax.axis_index(axis) == source, block, jnp.zeros_like(block))
    return lax.psum(block, axis)


def reducing(inverse_block, panels, pattern):
    row_count = lax.axis_size("row")
    col_count = lax.axis_size("col")
    row_index = lax.axis_index("row")
    col_index = lax.axis_index("col")
    rows_here = panels.shape[1]
    cols_here = inverse_block.shape[1]
    width = panels.shape[2]
    blocks = pattern.shape[1]
    block = rows_here * row_count // blocks
    ratio = col_count // row_count
    span = rows_here // col_count
    row_ids = row_index * rows_here + jnp.arange(rows_here, dtype=jnp.int32)
    onehot = (row_ids // block)[:, None] == jnp.arange(blocks, dtype=jnp.int32)[None, :]
    row_mask = jnp.sum(jnp.where(onehot[None, :, :], pattern[:, None, :], 0), axis=2)
    used = panels * row_mask[:, :, None].astype(jnp.bfloat16)
    piece = lax.dynamic_slice_in_dim(used, col_index % ratio * cols_here, cols_here, 1)
    col_panel = spread(piece, "row", col_index // ratio)
    product = jnp.einsum(
        "ij,sjw->siw", inverse_block, col_panel.astype(jnp.float32), precision=lax.Precision.HIGHEST
    )
    term = -(product * row_mask[:, :, None].astype(jnp.float32))
    share = width // col_count
    partial_update = jnp.einsum(
        "siv,siw->svw", used.astype(jnp.float32), term, precision=lax.Precision.HIGHEST
    )
    panel_parts = term.reshape(2, col_count, span, width)
    update_parts = partial_update.reshape(2, col_count, share, width)
    joined = jnp.concatenate([panel_parts, update_parts], axis=2).reshape(
        2, col_count * (span + share), width
    )
    received = lax.psum_scatter(joined, "col", scatter_dimension=1, tiled=True)
    inverse_panel = received[:, :span]
    update = -lax.psum(received[:, span:], "row")
    return (inverse_panel, update)


def halves(value):
    high = value.astype(jnp.bfloat16)
    return high, (value - high.astype(jnp.float32)).astype(jnp.bfloat16)


def pack_kernel(a_hbm, panels_hbm, a_out, last_out, panel_out, a_in, panel_in, sems):
    col = lax.axis_index("col")
    a_copy = pltpu.make_async_copy(a_hbm, a_in, sems.at[0])
    panel_copy = pltpu.make_async_copy(panels_hbm.at[col % 2], panel_in, sems.at[1])
    a_copy.start()
    panel_copy.start()
    a_copy.wait()
    packed = jnp.concatenate(halves(a_in[...]), axis=0)
    a_out[...] = packed
    last_out[0] = packed
    panel_copy.wait()
    for b in range(panel_out.shape[0]):
        panel_out[b] = panel_in[:, b * LANES : (b + 1) * LANES]
    last_out[1] = panel_in[:, pl.ds(pl.multiple_of(col // 2 * LANES, LANES), LANES)]


def arrange_kernel(own, first, second, last, mine, *rest):
    outs, turned = rest[:-1], rest[-1]
    tile = own.shape[0]
    row = lax.axis_index("row")
    chip = lax.axis_index("col") // 2
    chips = len(outs) + 1
    few = tile // chips
    mine[pl.ds(pl.multiple_of(row * tile, tile), tile), :] = own[...]
    mine[pl.ds(pl.multiple_of((row ^ 1) * tile, tile), tile), :] = first[...]
    mine[pl.ds(pl.multiple_of((row ^ 2) * tile, tile), tile), :] = second[...]
    mine[pl.ds(pl.multiple_of((row ^ 3) * tile, tile), tile), :] = last[0]
    mine[chips * tile : (chips + 1) * tile, :] = last[1]
    turned[...] = own[...].astype(jnp.float32).T
    here = pl.ds(pl.multiple_of(chip * few, few), few)
    mine[(chips + 1) * tile :, :] = turned[here, :].astype(jnp.bfloat16)
    for by, out in enumerate(outs, 1):
        other = chip ^ SECOND[by]
        out[:tile] = mine[pl.ds(pl.multiple_of(chip * tile, tile), tile), :]
        out[tile : 2 * tile] = mine[pl.ds(pl.multiple_of(other * tile, tile), tile), :]
        out[2 * tile : 3 * tile] = last[1]
        there = pl.ds(pl.multiple_of((chip ^ by) * few, few), few)
        out[3 * tile :] = turned[there, :].astype(jnp.bfloat16)


def local_kernel(pattern_ref, panels_ref, *refs):
    firsts, seconds = refs[:2], refs[2:4]
    owns, others = refs[4:6], refs[6:12]
    inverse_out, update_out, used, rhs, y, lhs = refs[12:]
    row = lax.axis_index("row")
    col = lax.axis_index("col")
    core = col % 2
    chip = col // 2
    rows, width = panels_ref.shape[1:]
    tile = rows
    half = tile // 2
    chips = width // tile
    share = update_out.shape[1]
    span = inverse_out.shape[1]
    block = used.shape[1] // pattern_ref.shape[1]
    sides = (core, 1 - core)

    def at(index, size):
        return pl.ds(pl.multiple_of(index * size, size), size)

    def keep(s, owner, lanes, read):
        for start in range(0, rows, block):
            flag = pattern_ref[s, (owner * rows + start) // block]
            value = read(pl.ds(start, block))
            to = pl.ds(pl.multiple_of(owner * rows + start, block), block)
            used[s, to, lanes] = jnp.where(flag != 0, value, jnp.zeros_like(value))

    for s in range(2):
        keep(s, row, slice(None), lambda r: panels_ref[s, r, :])
    for side in range(2):
        s = sides[side]
        for b in range(chips):
            lanes = pl.ds(b * LANES, LANES)
            keep(s, row ^ 1, lanes, lambda r: firsts[side][b, r, :])
            keep(s, row ^ 2, lanes, lambda r: seconds[side][b, r, :])
        keep(s, row ^ 3, at(chip, LANES), lambda r: owns[side][pl.ds(chips * tile + r.start, block), :])
        for by in range(1, chips):
            other = others[2 * (by - 1) + side]
            keep(s, row ^ 3, at(chip ^ by, LANES), lambda r: other[pl.ds(2 * tile + r.start, block), :])

    mine = at(chip, LANES)
    for s in range(2):
        rhs[:, s * LANES : (s + 1) * LANES] = used[s, :, mine]

    def dot(a, b):
        return jnp.dot(a, b, preferred_element_type=jnp.float32)

    def folded(which, side, value):
        to = pl.ds(pl.multiple_of(which * tile + sides[side] * half, half), half)
        start = side * tile
        return to, value[start : start + half] + value[start + half : start + tile]

    def twice(which):
        pieces = []
        for side in range(2):
            piece = rhs[pl.ds(pl.multiple_of(which * tile + sides[side] * half, half), half), :]
            pieces += [piece, piece]
        return pieces

    def turn(ref, start):
        return ref[start, :].T

    stack = jnp.concatenate(
        [
            jnp.concatenate([owns[side][i * tile : (i + 1) * tile, :] for i in range(chips)], axis=1)
            for side in range(2)
        ],
        axis=0,
    )
    value = dot(stack, rhs[...])
    for side in range(2):
        to, part = folded(chip, side, value)
        y[to, :] = part
    own_twice = twice(chip)
    for by in range(1, chips):
        pair = others[2 * (by - 1) : 2 * by]
        which = chip ^ by
        source = SOURCE[by]
        far = others[2 * (source - 1) : 2 * source]
        turned = [turn(owns[side], at(which, tile)) for side in range(2)]
        turned += [turn(far[side], pl.ds(tile, tile)) for side in range(2)]
        y[at(which, tile), :] = dot(
            jnp.concatenate(turned, axis=1),
            jnp.concatenate(own_twice + twice(chip ^ source), axis=0),
        )
        stack = jnp.concatenate(
            [
                jnp.concatenate([pair[side][:tile, :], pair[side][tile : 2 * tile, :]], axis=1)
                for side in range(2)
            ],
            axis=0,
        )
        value = dot(
            stack,
            jnp.concatenate([rhs[at(which, tile), :], rhs[at(which ^ SECOND[by], tile), :]], axis=0),
        )
        for side in range(2):
            to, part = folded(which, side, value)
            y[to, :] += part

    for by in range(chips):
        if by == 0:
            pair, start = owns, (chips + 1) * tile
        else:
            pair, start = others[2 * (by - 1) : 2 * by], 3 * tile
        a, b = [
            pair[side][pl.ds(pl.multiple_of(start + core * span, span), span), :].astype(jnp.float32)
            for side in range(2)
        ]
        a, b = jnp.where(core == 0, a, b), jnp.where(core == 0, b, a)
        lanes = at(chip ^ by, LANES)
        high = jnp.concatenate([a[:, :half], b[:, :half]], axis=1)
        low = jnp.concatenate([a[:, half:], b[:, half:]], axis=1)
        lhs[2 * share : 2 * share + span, lanes] = high.astype(jnp.bfloat16)
        lhs[2 * share + span :, lanes] = low.astype(jnp.bfloat16)

    for s in range(2):
        y_t = y[:, s * LANES : (s + 1) * LANES].T
        high, low = halves(jnp.where(core == 0, y_t[:share], y_t[share:]))
        lhs[:share] = high
        lhs[share : 2 * share] = low
        out = dot(lhs[...], used[s])
        update_out[s] = out[:share] + out[share : 2 * share]
        flag = pattern_ref[s, (row * rows + col * span) // block]
        product = out[2 * share : 2 * share + span] + out[2 * share + span :]
        inverse_out[s] = jnp.where(flag != 0, -product, jnp.zeros_like(product))


def gathering(inverse_block, panels, pattern):
    return gathered(inverse_block, panels, pattern)


def gathered(inverse_block, panels, pattern):
    col_count = lax.axis_size("col")
    _, rows, width = panels.shape
    tile = rows
    chips = col_count // 2
    height = rows * lax.axis_size("row")
    cols = inverse_block.shape[1]
    share = width // col_count
    span = rows // col_count
    vmem = pl.BlockSpec(memory_space=pltpu.VMEM)
    hbm = pl.BlockSpec(memory_space=pltpu.HBM)
    params = pltpu.CompilerParams(vmem_limit_bytes=KERNEL_VMEM)

    def bf16(*shape):
        return jax.ShapeDtypeStruct(shape, jnp.bfloat16)

    def swap(value, axis, by):
        return lax.ppermute(value, axis, [(i, i ^ by) for i in range(lax.axis_size(axis))])

    a, last, panel = pl.pallas_call(
        pack_kernel,
        out_shape=(bf16(tile, LANES), bf16(2, tile, LANES), bf16(chips, tile, LANES)),
        in_specs=[hbm] * 2,
        out_specs=(vmem,) * 3,
        scratch_shapes=[
            pltpu.VMEM((cols, rows), jnp.float32),
            pltpu.VMEM((rows, width), jnp.bfloat16),
            pltpu.SemaphoreType.DMA((2,)),
        ],
        compiler_params=PACK_PARAMS,
    )(inverse_block.T, panels)
    second_a = swap(a, "row", 2)
    last = swap(last, "row", 3)
    first_a = swap(a, "row", 1)
    second = swap(panel, "row", 2)
    first = swap(panel, "row", 1)
    few = tile // chips
    own, *sent = pl.pallas_call(
        arrange_kernel,
        out_shape=(bf16((chips + 1) * tile + few, LANES),) + (bf16(3 * tile + few, LANES),) * (chips - 1),
        in_specs=[vmem] * 4,
        out_specs=(vmem,) * chips,
        scratch_shapes=[pltpu.VMEM((tile, LANES), jnp.float32)],
        compiler_params=params,
    )(a, first_a, second_a, last)
    others = []
    for by, value in enumerate(sent, 1):
        value = swap(value, "col", 2 * by)
        others += [value, swap(value, "col", 1)]
    return pl.pallas_call(
        local_kernel,
        out_shape=(
            jax.ShapeDtypeStruct((2, span, width), jnp.float32),
            jax.ShapeDtypeStruct((2, share, width), jnp.float32),
        ),
        in_specs=[pl.BlockSpec(memory_space=pltpu.SMEM)] + [vmem] * (7 + 2 * (chips - 1)),
        out_specs=(vmem,) * 2,
        scratch_shapes=[
            pltpu.VMEM((2, height, width), jnp.bfloat16),
            pltpu.VMEM((height, 2 * LANES), jnp.bfloat16),
            pltpu.VMEM((height, 2 * LANES), jnp.float32),
            pltpu.VMEM((2 * share + 2 * span, height), jnp.bfloat16),
        ],
        compiler_params=params,
    )(pattern, panels, first, swap(first, "col", 1), second, swap(second, "col", 1), own, swap(own, "col", 1), *others)


def fits(mesh, inverse_block, panels, pattern):
    row_count, col_count = mesh.shape["row"], mesh.shape["col"]
    height, width = inverse_block.shape[0], panels.shape[2]
    rows, cols = height // row_count, height // col_count
    block = height // pattern.shape[1]
    return (
        row_count == len(SECOND) + 1
        and col_count == 2 * row_count
        and width == LANES * row_count
        and inverse_block.size * 4 <= LOCAL_BYTES
        and 2 * cols == LANES
        and 2 * (width // col_count) == LANES
        and rows == 2 * cols
        and rows % block == 0
        and block % 16 == 0
        and (rows // col_count) % 16 == 0
    )


def solution(mesh):
    def run(inverse_block, panels, pattern):
        body = gathering if fits(mesh, inverse_block, panels, pattern) else reducing
        mapped = jax.shard_map(
            body,
            mesh=mesh,
            in_specs=(P("row", "col"), P(None, "row", None), P()),
            out_specs=(P(None, ("row", "col"), None), P(None, "col", None)),
            check_vma=False,
        )
        return mapped(inverse_block, panels, pattern)

    return run
```
